256 devices in a mesh: dp: 32 (over z_hi, y, core), tensor: 8 (over x, z_lo).
Axes of the slice: x: 4, y: 4, z: 8 (z_hi: 4, z_lo: 2; z = z_hi * 2 + z_lo), core: 2. Of those that a mesh axis runs over, the one named last changes fastest.
Arguments:
- hidden: bfloat16 [32, 1024, 28672], P('dp', None, 'tensor'), may hold values from -6 to 6
- grad_out: bfloat16 [32, 1024, 8192], P('dp', None, 'tensor'), may hold values from -30 to 30
- proj_in: bfloat16 [64, 28672], P(None, 'tensor'), may hold values from -0.03125 to 0.03125
- proj_out: bfloat16 [64, 8192], P(None, 'tensor'), may hold values from -0.0625 to 0.0625
Outputs:
- covariance: float32 [4096, 4096], P('dp', 'tensor')
The draws below stay inside these ranges and needn't reach their ends.
All inputs are finite; a program needn't handle non-finite values.
Results may differ from the reference program's by a relative error of at most 0.0003.
Values sent between devices are 32-bit elements; how exact they have to be, the bound alone decides.
No kernel may reach another device: no remote copies, remote signals or barrier semaphores. Data moves between devices by JAX's collectives and lax.ppermute only.
A program may use at most 64 MiB of HBM per device.

```python
import math
import jax
import jax.numpy as jnp
from jax import lax

D = 8192
FF = 28672
K = 64
SEQ_LEN = 1024
SEQS = 32
KK = 4096


def draw_grad_out(key, part):
    steps = jnp.arange(SEQS, dtype=jnp.float32) / (SEQS - 1)
    base = jax.random.truncated_normal(key, -6.0, 6.0, (SEQS, SEQ_LEN, D), jnp.float32)
    rising = 3.0 ** steps
    return (base * rising[:, None, None]).astype(jnp.bfloat16)


def shard_levels(own_key, shape, shards, low, largest):
    factor_of = 1.0
    for dim, blocks in shards:
        steps = jax.random.uniform(jax.random.fold_in(jax.random.fold_in(own_key, 6), dim), (blocks,), jnp.float32, low / len(shards), largest / len(shards))
        factor_of = factor_of * jnp.repeat(jnp.exp(steps), shape[dim] // blocks).reshape((-1,) + (1,) * (len(shape) - 1 - dim))
    return factor_of


def bell_draw(own_key, shape, spread, reach, shards=(), kind=jnp.bfloat16):
    array = jax.random.normal(own_key, shape, jnp.float32) * spread
    if len(shards) > 0:
        array = shard_levels(own_key, shape, shards, -0.22, 0.18) * array
    return jnp.clip(array, min=-reach, max=reach).astype(kind)


def setup_inputs(seed: int = 0) -> dict:
    splits = jax.random.split(jax.random.key(seed), 5)
    hidden = bell_draw(splits[0], (SEQS, SEQ_LEN, FF), 1.0, 6.0, ((0, 32), (2, 8)))
    grad_out = draw_grad_out(jax.random.fold_in(splits[4], 71), 0)
    proj_in = bell_draw(splits[2], (K, FF), FF ** -0.5, 0.03125, ((1, 8),))
    proj_out = bell_draw(splits[3], (K, D), D ** -0.5, 0.0625, ((1, 8),))
    return {"hidden": hidden, "grad_out": grad_out, "proj_in": proj_in, "proj_out": proj_out}


def reference(hidden, grad_out, proj_in, proj_out):
    inv_root = 1.0 / math.sqrt(SEQ_LEN)

    def one_sequence(seq_pair):
        seq_hidden, seq_grad = seq_pair
        in_panel = jnp.dot(seq_hidden, proj_in.T, preferred_element_type=jnp.float32)
        out_panel = jnp.dot(seq_grad, proj_out.T, preferred_element_type=jnp.float32)
        outer = jnp.dot(in_panel.T, out_panel, precision=lax.Precision.HIGHEST, preferred_element_type=jnp.float32)
        return (outer * inv_root).reshape(-1)
    seq_grads = lax.map(one_sequence, (hidden, grad_out))
    raw_cov = jnp.dot(seq_grads.T, seq_grads, precision=lax.Precision.HIGHEST, preferred_element_type=jnp.float32) / SEQS
    damping = 0.5 * jnp.sum(seq_grads * seq_grads) / (SEQS * KK)
    return raw_cov + damping * jnp.eye(KK, dtype=jnp.float32)
```

```python
import math

import jax
import jax.numpy as jnp
from jax import lax
from jax.sharding import Mesh, PartitionSpec as P

DP = ("zh", "y", "c")
TENSOR = ("x", "zl")


def shards(hidden, grad_out, proj_in, proj_out):
    length = hidden.shape[1]
    width = proj_in.shape[0]
    inv_root = 1.0 / math.sqrt(length)
    tensor = lax.axis_size(TENSOR)
    outer_dp = lax.axis_size(("zh", "y"))
    cores = lax.axis_size("c")
    seqs = outer_dp * cores
    t = lax.axis_index(TENSOR)
    d = lax.axis_index(DP)
    core = lax.axis_index("c")
    col_as = width // tensor
    row_as = width // seqs

    in_panel = jnp.einsum("tf,af->ta", hidden[0], proj_in, preferred_element_type=jnp.float32)
    out_panel = jnp.einsum("te,be->tb", grad_out[0], proj_out, preferred_element_type=jnp.float32)
    panels = jnp.concatenate([in_panel, out_panel], axis=1)

    parts = lax.all_to_all(panels.reshape(tensor, length // tensor, 2 * width), TENSOR, 0, 0)
    mine = jnp.sum(parts, axis=0)
    partial = lax.dot_general(
        mine[:, :width], mine[:, width:], (((0,), (0,)), ((), ())),
        precision=lax.Precision.HIGHEST, preferred_element_type=jnp.float32,
    ) * inv_root

    copies = jnp.broadcast_to(partial[None], (tensor, width, width))
    grads = jnp.sum(lax.all_to_all(copies, TENSOR, 0, 0), axis=0)

    pair = lax.all_gather(grads, "c")
    squares = jnp.sum(pair * pair, axis=(1, 2))

    cols = lax.dynamic_slice_in_dim(pair, t * col_as, col_as, 1)
    rows = pair.reshape(cores, outer_dp, cores, row_as, width)
    rows = lax.dynamic_index_in_dim(rows, core, 2, keepdims=False)
    rows = rows.transpose(1, 0, 2, 3)
    cols = jnp.broadcast_to(cols[None], (outer_dp, cores, col_as, width))
    squares = jnp.broadcast_to(squares[None, :, None, None], (outer_dp, cores, 1, width))
    sent = jnp.concatenate([cols, rows, squares], axis=2)
    got = lax.all_to_all(sent, ("zh", "y"), 0, 0)
    got = got.reshape(seqs, col_as + row_as + 1, width)
    col_block = got[:, :col_as].reshape(seqs, col_as * width)
    row_block = got[:, col_as:col_as + row_as].reshape(seqs, row_as * width)
    trace_total = jnp.sum(got[:, col_as + row_as, 0])

    raw_block = lax.dot_general(
        row_block, col_block, (((0,), (0,)), ((), ())),
        precision=lax.Precision.HIGHEST, preferred_element_type=jnp.float32,
    )
    total_len = width * width
    damping = 0.5 * trace_total / (seqs * total_len)
    row_count, col_count = raw_block.shape
    row_ids = d * row_count + lax.broadcasted_iota(jnp.int32, (row_count, col_count), 0)
    col_ids = t * col_count + lax.broadcasted_iota(jnp.int32, (row_count, col_count), 1)
    return raw_block / seqs + jnp.where(row_ids == col_ids, damping, jnp.float32(0.0))


def solution(mesh):
    fine = Mesh(mesh.devices.reshape(4, 4, 2, 4, 2), ("zh", "y", "c", "x", "zl"))
    placed = (
        P(DP, None, TENSOR),
        P(DP, None, TENSOR),
        P(None, TENSOR),
        P(None, TENSOR),
    )
    return jax.shard_map(
        shards, mesh=fine, in_specs=placed, out_specs=P(DP, TENSOR), check_vma=False
    )
```

```python
import functools
import math

import jax
import jax.numpy as jnp
from jax import lax
from jax.experimental import pallas as pl
from jax.experimental.pallas import tpu as pltpu
from jax.sharding import Mesh, PartitionSpec as P

DP = ("zh", "y", "c")
TENSOR = ("x", "zl")
LANES = 128
GRAD_BLOCKS = (1024,)
HIDDEN_BLOCKS = (1024, 1024, 1536)
AHEAD = 2
VMEM_LIMIT = 25165824
F32 = jnp.float32


def panels_kernel(hidden, grad_out, proj_in, proj_out, panels, h_buf, g_buf, p_buf, q_buf, sems, proj_sems):
    width = proj_in.shape[0]
    across = (((1,), (1,)), ((), ()))
    proj_copies = (
        pltpu.make_async_copy(proj_out, q_buf, proj_sems.at[0]),
        pltpu.make_async_copy(proj_in, p_buf, proj_sems.at[1]),
    )
    work = []
    for source, buf, proj, lanes, eighths in (
        (grad_out, g_buf, q_buf, pl.ds(width, width), GRAD_BLOCKS),
        (hidden, h_buf, p_buf, pl.ds(0, width), HIDDEN_BLOCKS),
    ):
        begin = 0
        for size in eighths:
            span = pl.ds(begin, size)
            copy = pltpu.make_async_copy(source.at[:, span], buf.at[:, span], sems.at[len(work)])
            work.append((copy, buf, proj, lanes, span, begin == 0))
            begin += size
        assert begin == source.shape[1]
    for copy in proj_copies:
        copy.start()
    for item in work[:AHEAD]:
        item[0].start()
    for copy in proj_copies:
        copy.wait()
    for k, (copy, buf, proj, lanes, span, first) in enumerate(work):
        copy.wait()
        if k + AHEAD < len(work):
            work[k + AHEAD][0].start()
        part = lax.dot_general(buf[:, span], proj[:, span], across, preferred_element_type=F32)
        panels[:, lanes] = part if first else panels[:, lanes] + part


def make_panels(hidden, grad_out, proj_in, proj_out):
    length, units = hidden.shape
    features = grad_out.shape[1]
    width = proj_in.shape[0]
    blocks = len(GRAD_BLOCKS) + len(HIDDEN_BLOCKS)
    hbm = pl.BlockSpec(memory_space=pltpu.HBM)
    return pl.pallas_call(
        panels_kernel,
        out_shape=jax.ShapeDtypeStruct((length, 2 * width), F32),
        in_specs=[hbm] * 4,
        out_specs=pl.BlockSpec(memory_space=pltpu.VMEM),
        scratch_shapes=[
            pltpu.VMEM((length, units), jnp.bfloat16),
            pltpu.VMEM((length, features), jnp.bfloat16),
            pltpu.VMEM((width, units), jnp.bfloat16),
            pltpu.VMEM((width, features), jnp.bfloat16),
            pltpu.SemaphoreType.DMA((blocks,)),
            pltpu.SemaphoreType.DMA((2,)),
        ],
        compiler_params=pltpu.CompilerParams(vmem_limit_bytes=VMEM_LIMIT),
        name="panels",
    )(hidden, grad_out, proj_in, proj_out)


def outer_kernel(parts, copies, square, *, scale):
    width = square.shape[0]
    mine = jnp.sum(parts[...], axis=0)
    square[...] = lax.dot_general(
        mine[:, :width], mine[:, width:], (((0,), (0,)), ((), ())),
        precision=lax.Precision.HIGHEST, preferred_element_type=F32,
    ) * scale
    half = width // 2
    flat = jnp.concatenate([square[pl.ds(0, half, stride=2), :], square[pl.ds(1, half, stride=2), :]], axis=1)
    for k in range(copies.shape[0]):
        copies[k] = flat


def make_outer(parts, width, receivers, scale):
    return pl.pallas_call(
        functools.partial(outer_kernel, scale=scale),
        out_shape=jax.ShapeDtypeStruct((receivers, width // 2, 2 * width), F32),
        in_specs=[pl.BlockSpec(memory_space=pltpu.VMEM)],
        out_specs=pl.BlockSpec(memory_space=pltpu.VMEM),
        scratch_shapes=[pltpu.VMEM((width, width), F32)],
        compiler_params=pltpu.CompilerParams(vmem_limit_bytes=8 << 20),
        name="outer",
    )(parts)


def pack_kernel(partial, sent, grads, *, tensor, cores, col_rows):
    t = lax.axis_index(TENSOR).astype(jnp.int32)
    core = lax.axis_index("c").astype(jnp.int32)
    chips = sent.shape[0]
    for c in range(cores):
        g = partial[c]
        for k in range(1, tensor):
            g = g + partial[k * cores + c]
        grads[c] = g
        total = jnp.broadcast_to(jnp.sum(g * g), (1, LANES))
        cols = grads[c, pl.ds(t * col_rows, col_rows), :]
        for k in range(chips):
            sent[k, pl.ds(8 * c, col_rows), :] = cols
            sent[k, pl.ds(8 * c + col_rows, 1), :] = grads[c, pl.ds(k * cores + core, 1), :]
            sent[k, pl.ds(8 * c + col_rows + 1, 1), :] = total


def make_sent(partial, tensor, cores, chips, col_rows):
    rows = partial.shape[1]
    return pl.pallas_call(
        functools.partial(pack_kernel, tensor=tensor, cores=cores, col_rows=col_rows),
        out_shape=jax.ShapeDtypeStruct((chips, 8 * cores, LANES), F32),
        in_specs=[pl.BlockSpec(memory_space=pltpu.VMEM)],
        out_specs=pl.BlockSpec(memory_space=pltpu.VMEM),
        scratch_shapes=[pltpu.VMEM((cores, rows, LANES), F32)],
        compiler_params=pltpu.CompilerParams(vmem_limit_bytes=8 << 20),
        name="pack",
    )(partial)


def cov_kernel(got, out, *, col_rows, seqs, total_len):
    row_begin = lax.axis_index(DP).astype(jnp.int32) * out.shape[0]
    col_begin = lax.axis_index(TENSOR).astype(jnp.int32) * out.shape[1]
    cols = jnp.concatenate([got[pl.ds(q, seqs, stride=8), :] for q in range(col_rows)], axis=1)
    rows = got[pl.ds(col_rows, seqs, stride=8), :]
    totals = got[pl.ds(col_rows + 1, seqs, stride=8), :]
    damping = (0.5 / (seqs * total_len)) * jnp.sum(totals, axis=0, keepdims=True)[:, :1]
    raw = lax.dot_general(
        rows, cols, (((0,), (0,)), ((), ())), precision=lax.Precision.HIGHEST, preferred_element_type=F32
    ) * (1.0 / seqs)
    row_ids = row_begin + lax.broadcasted_iota(jnp.int32, raw.shape, 0)
    col_ids = col_begin + lax.broadcasted_iota(jnp.int32, raw.shape, 1)
    out[...] = raw + jnp.where(row_ids == col_ids, damping, 0.0)


def make_cov(got, col_rows, seqs, total_len):
    return pl.pallas_call(
        functools.partial(cov_kernel, col_rows=col_rows, seqs=seqs, total_len=total_len),
        out_shape=jax.ShapeDtypeStruct((LANES, col_rows * LANES), F32),
        in_specs=[pl.BlockSpec(memory_space=pltpu.VMEM)],
        out_specs=pl.BlockSpec(memory_space=pltpu.VMEM),
        compiler_params=pltpu.CompilerParams(vmem_limit_bytes=8 << 20),
        name="cov",
    )(got)


def shards(hidden, grad_out, proj_in, proj_out):
    length = hidden.shape[1]
    width = proj_in.shape[0]
    total_len = width * width
    tensor = lax.axis_size(TENSOR)
    chips = lax.axis_size(("zh", "y"))
    cores = lax.axis_size("c")
    seqs = chips * cores
    col_rows = total_len // tensor // LANES

    panels = make_panels(*(pltpu.with_memory_space_constraint(v, pltpu.HBM) for v in (hidden[0], grad_out[0], proj_in, proj_out)))
    parts = lax.all_to_all(panels.reshape(tensor, length // tensor, 2 * width), TENSOR, 0, 0)
    copies = make_outer(parts, width, tensor * cores, 1.0 / math.sqrt(length))
    partial = lax.all_to_all(copies, (*TENSOR, "c"), 0, 0)
    sent = make_sent(partial, tensor, cores, chips, col_rows)
    got = lax.all_to_all(sent, ("zh", "y"), 0, 0)
    return make_cov(got.reshape(seqs * 8, LANES), col_rows, seqs, total_len)


def solution(mesh):
    fine = Mesh(mesh.devices.reshape(4, 4, 2, 4, 2), ("zh", "y", "c", "x", "zl"))
    placed = (
        P(DP, None, TENSOR),
        P(DP, None, TENSOR),
        P(None, TENSOR),
        P(None, TENSOR),
    )
    return jax.shard_map(
        shards, mesh=fine, in_specs=placed, out_specs=P(DP, TENSOR), check_vma=False
    )
```

```python
import functools
import math

import jax
import jax.numpy as jnp
from jax import lax
from jax.experimental import pallas as pl
from jax.experimental.pallas import tpu as pltpu
from jax.sharding import Mesh, PartitionSpec as P

DP = ("zh", "y", "c")
TENSOR = ("x", "zl")
LANES = 128
GRAD_BLOCKS = (512, 512)
HIDDEN_BLOCKS = (1536, 1024, 1024)
AHEAD = 3
ROWS = 256
VMEM_LIMIT = 25165824
F32 = jnp.float32


def panels_kernel(hidden, grad_out, proj_in, proj_out, panels, h_buf, g_buf, p_buf, q_buf, sems, proj_sems):
    width = proj_in.shape[0]
    across = (((1,), (1,)), ((), ()))
    proj_copies = (
        pltpu.make_async_copy(proj_out, q_buf, proj_sems.at[0]),
        pltpu.make_async_copy(proj_in, p_buf, proj_sems.at[1]),
    )
    work = []
    for source, buf, proj, lanes, eighths in (
        (grad_out, g_buf, q_buf, pl.ds(width, width), GRAD_BLOCKS),
        (hidden, h_buf, p_buf, pl.ds(0, width), HIDDEN_BLOCKS),
    ):
        begin = 0
        for size in eighths:
            span = pl.ds(begin, size)
            copy = pltpu.make_async_copy(source.at[:, span], buf.at[:, span], sems.at[len(work)])
            work.append((copy, buf, proj, lanes, span, begin == 0))
            begin += size
        assert begin == source.shape[1]
    for copy in proj_copies:
        copy.start()
    for item in work[:AHEAD]:
        item[0].start()
    for copy in proj_copies:
        copy.wait()
    for k, (copy, buf, proj, lanes, span, first) in enumerate(work):
        copy.wait()
        if k + AHEAD < len(work):
            work[k + AHEAD][0].start()
        for r in range(0, panels.shape[0], ROWS):
            rows = pl.ds(r, ROWS)
            part = lax.dot_general(buf[rows, span], proj[:, span], across, preferred_element_type=F32)
            panels[rows, lanes] = part if first else panels[rows, lanes] + part


def make_panels(hidden, grad_out, proj_in, proj_out):
    length, units = hidden.shape
    features = grad_out.shape[1]
    width = proj_in.shape[0]
    blocks = len(GRAD_BLOCKS) + len(HIDDEN_BLOCKS)
    hbm = pl.BlockSpec(memory_space=pltpu.HBM)
    return pl.pallas_call(
        panels_kernel,
        out_shape=jax.ShapeDtypeStruct((length, 2 * width), F32),
        in_specs=[hbm] * 4,
        out_specs=pl.BlockSpec(memory_space=pltpu.VMEM),
        scratch_shapes=[
            pltpu.VMEM((length, units), jnp.bfloat16),
            pltpu.VMEM((length, features), jnp.bfloat16),
            pltpu.VMEM((width, units), jnp.bfloat16),
            pltpu.VMEM((width, features), jnp.bfloat16),
            pltpu.SemaphoreType.DMA((blocks,)),
            pltpu.SemaphoreType.DMA((2,)),
        ],
        compiler_params=pltpu.CompilerParams(vmem_limit_bytes=VMEM_LIMIT),
        name="panels",
    )(hidden, grad_out, proj_in, proj_out)


def outer_kernel(parts, copies, square, *, scale):
    width = square.shape[0]
    mine = jnp.sum(parts[...], axis=0)
    square[...] = lax.dot_general(
        mine[:, :width], mine[:, width:], (((0,), (0,)), ((), ())),
        precision=lax.Precision.HIGHEST, preferred_element_type=F32,
    ) * scale
    half = width // 2
    flat = jnp.concatenate([square[pl.ds(0, half, stride=2), :], square[pl.ds(1, half, stride=2), :]], axis=1)
    for k in range(copies.shape[0]):
        copies[k] = flat


def make_outer(parts, width, receivers, scale):
    return pl.pallas_call(
        functools.partial(outer_kernel, scale=scale),
        out_shape=jax.ShapeDtypeStruct((receivers, width // 2, 2 * width), F32),
        in_specs=[pl.BlockSpec(memory_space=pltpu.VMEM)],
        out_specs=pl.BlockSpec(memory_space=pltpu.VMEM),
        scratch_shapes=[pltpu.VMEM((width, width), F32)],
        compiler_params=pltpu.CompilerParams(vmem_limit_bytes=8 << 20),
        name="outer",
    )(parts)


def pack_kernel(partial, sent, grads, *, tensor, cores, col_rows):
    t = lax.axis_index(TENSOR).astype(jnp.int32)
    core = lax.axis_index("c").astype(jnp.int32)
    each = slot_rows(cores, col_rows)
    squares = []
    for c in range(cores):
        g = partial[c]
        for k in range(1, tensor):
            g = g + partial[k * cores + c]
        grads[c] = g
        squares.append(g * g)
    fill = each - cores * (col_rows + 1)
    total = jnp.broadcast_to(jnp.sum(sum(squares)), (fill, LANES))
    for k in range(sent.shape[0] // each):
        for c in range(cores):
            sent[pl.ds(k * each + c * col_rows, col_rows), :] = grads[c, pl.ds(t * col_rows, col_rows), :]
            sent[pl.ds(k * each + cores * col_rows + c, 1), :] = grads[c, pl.ds(k * cores + core, 1), :]
        sent[pl.ds((k + 1) * each - fill, fill), :] = total


def slot_rows(cores, col_rows):
    return cores * col_rows + 4


def make_sent(partial, tensor, cores, chips, col_rows):
    rows = partial.shape[1]
    return pl.pallas_call(
        functools.partial(pack_kernel, tensor=tensor, cores=cores, col_rows=col_rows),
        out_shape=jax.ShapeDtypeStruct((chips * slot_rows(cores, col_rows), LANES), F32),
        in_specs=[pl.BlockSpec(memory_space=pltpu.VMEM)],
        out_specs=pl.BlockSpec(memory_space=pltpu.VMEM),
        scratch_shapes=[pltpu.VMEM((cores, rows, LANES), F32)],
        compiler_params=pltpu.CompilerParams(vmem_limit_bytes=8 << 20),
        name="pack",
    )(partial)


def cov_kernel(got, out, block, sems, *, cores, col_rows, seqs, total_len):
    each = slot_rows(cores, col_rows)
    chips = seqs // cores
    row_begin = lax.axis_index(DP).astype(jnp.int32) * out.shape[0]
    col_begin = lax.axis_index(TENSOR).astype(jnp.int32) * out.shape[1]

    def over_seqs(first, step):
        slots = [got[pl.ds(first + c * step, chips, stride=each), :] for c in range(cores)]
        return jnp.concatenate(slots, axis=0)

    rows = over_seqs(cores * col_rows, 1)
    totals = got[pl.ds(cores * (col_rows + 1), chips, stride=each), :]
    damping = (0.5 / (seqs * total_len)) * jnp.sum(totals, axis=0, keepdims=True)
    row_ids = row_begin + lax.broadcasted_iota(jnp.int32, (out.shape[0], LANES), 0)
    lane_ids = col_begin + lax.broadcasted_iota(jnp.int32, (out.shape[0], LANES), 1)
    copies = []
    for q in range(col_rows):
        raw = lax.dot_general(
            rows, over_seqs(q, col_rows), (((0,), (0,)), ((), ())),
            precision=lax.Precision.HIGHEST, preferred_element_type=F32,
        )
        block[q] = raw * (1.0 / seqs) + jnp.where(row_ids == lane_ids + q * LANES, damping, 0.0)
        copies.append(pltpu.make_async_copy(block.at[q], out.at[:, pl.ds(q * LANES, LANES)], sems.at[q]))
        copies[q].start()
    for copy in copies:
        copy.wait()


def make_cov(got, cores, col_rows, seqs, total_len):
    return pl.pallas_call(
        functools.partial(cov_kernel, cores=cores, col_rows=col_rows, seqs=seqs, total_len=total_len),
        out_shape=jax.ShapeDtypeStruct((LANES, col_rows * LANES), F32),
        in_specs=[pl.BlockSpec(memory_space=pltpu.VMEM)],
        out_specs=pl.BlockSpec(memory_space=pltpu.HBM),
        scratch_shapes=[pltpu.VMEM((col_rows, LANES, LANES), F32), pltpu.SemaphoreType.DMA((col_rows,))],
        compiler_params=pltpu.CompilerParams(vmem_limit_bytes=8 << 20),
        name="cov",
    )(got)


def shards(hidden, grad_out, proj_in, proj_out):
    length = hidden.shape[1]
    width = proj_in.shape[0]
    total_len = width * width
    tensor = lax.axis_size(TENSOR)
    chips = lax.axis_size(("zh", "y"))
    cores = lax.axis_size("c")
    seqs = chips * cores
    col_rows = total_len // tensor // LANES
    each = slot_rows(cores, col_rows)

    panels = make_panels(*(pltpu.with_memory_space_constraint(v, pltpu.HBM) for v in (hidden[0], grad_out[0], proj_in, proj_out)))
    parts = lax.all_to_all(panels.reshape(tensor, length // tensor, 2 * width), TENSOR, 0, 0)
    copies = make_outer(parts, width, tensor * cores, 1.0 / math.sqrt(length))
    partial = lax.all_to_all(copies, (*TENSOR, "c"), 0, 0)
    sent = make_sent(partial, tensor, cores, chips, col_rows)
    got = lax.all_to_all(sent.reshape(chips, each // 4, 4, LANES), ("zh", "y"), 0, 0)
    return make_cov(got.reshape(chips * each, LANES), cores, col_rows, seqs, total_len)


def solution(mesh):
    fine = Mesh(mesh.devices.reshape(4, 4, 2, 4, 2), ("zh", "y", "c", "x", "zl"))
    placed = (
        P(DP, None, TENSOR),
        P(DP, None, TENSOR),
        P(None, TENSOR),
        P(None, TENSOR),
    )
    return jax.shard_map(
        shards, mesh=fine, in_specs=placed, out_specs=P(DP, TENSOR), check_vma=False
    )
```

```python
import functools
import math

import jax
import jax.numpy as jnp
from jax import lax
from jax.experimental import pallas as pl
from jax.experimental.pallas import tpu as pltpu
from jax.sharding import Mesh, PartitionSpec as P

DP = ("p", "c")
TENSOR = "t"
LANES = 128
P_ORDER = [10, 0, 1, 3, 2, 4, 5, 7, 6, 12, 8, 13, 15, 14, 9, 11]
T_ORDER = [5, 7, 4, 3, 6, 2, 1, 0]
GRAD_BLOCKS = (512, 512)
HIDDEN_BLOCKS = (1536, 1024, 1024)
AHEAD = 3
ROWS = 256
VMEM_LIMIT = 25165824
F32 = jnp.float32


def panels_kernel(hidden, grad_out, proj_in, proj_out, panels, h_buf, g_buf, p_buf, q_buf, sems, proj_sems):
    width = proj_in.shape[0]
    across = (((1,), (1,)), ((), ()))
    proj_copies = (
        pltpu.make_async_copy(proj_out, q_buf, proj_sems.at[0]),
        pltpu.make_async_copy(proj_in, p_buf, proj_sems.at[1]),
    )
    work = []
    for source, buf, proj, lanes, eighths in (
        (grad_out, g_buf, q_buf, pl.ds(width, width), GRAD_BLOCKS),
        (hidden, h_buf, p_buf, pl.ds(0, width), HIDDEN_BLOCKS),
    ):
        begin = 0
        for size in eighths:
            span = pl.ds(begin, size)
            copy = pltpu.make_async_copy(source.at[:, span], buf.at[:, span], sems.at[len(work)])
            work.append((copy, buf, proj, lanes, span, begin == 0))
            begin += size
        assert begin == source.shape[1]
    for copy in proj_copies:
        copy.start()
    for item in work[:AHEAD]:
        item[0].start()
    for copy in proj_copies:
        copy.wait()
    for k, (copy, buf, proj, lanes, span, first) in enumerate(work):
        copy.wait()
        if k + AHEAD < len(work):
            work[k + AHEAD][0].start()
        for r in range(0, panels.shape[0], ROWS):
            rows = pl.ds(r, ROWS)
            part = lax.dot_general(buf[rows, span], proj[:, span], across, preferred_element_type=F32)
            panels[rows, lanes] = part if first else panels[rows, lanes] + part


def make_panels(hidden, grad_out, proj_in, proj_out):
    length, units = hidden.shape
    features = grad_out.shape[1]
    width = proj_in.shape[0]
    blocks = len(GRAD_BLOCKS) + len(HIDDEN_BLOCKS)
    hbm = pl.BlockSpec(memory_space=pltpu.HBM)
    return pl.pallas_call(
        panels_kernel,
        out_shape=jax.ShapeDtypeStruct((length, 2 * width), F32),
        in_specs=[hbm] * 4,
        out_specs=pl.BlockSpec(memory_space=pltpu.VMEM),
        scratch_shapes=[
            pltpu.VMEM((length, units), jnp.bfloat16),
            pltpu.VMEM((length, features), jnp.bfloat16),
            pltpu.VMEM((width, units), jnp.bfloat16),
            pltpu.VMEM((width, features), jnp.bfloat16),
            pltpu.SemaphoreType.DMA((blocks,)),
            pltpu.SemaphoreType.DMA((2,)),
        ],
        compiler_params=pltpu.CompilerParams(vmem_limit_bytes=VMEM_LIMIT),
        name="panels",
    )(hidden, grad_out, proj_in, proj_out)


def outer_kernel(parts, copies, square, *, scale):
    width = square.shape[0]
    mine = jnp.sum(parts[...], axis=0)
    square[...] = lax.dot_general(
        mine[:, :width], mine[:, width:], (((0,), (0,)), ((), ())),
        precision=lax.Precision.HIGHEST, preferred_element_type=F32,
    ) * scale
    half = width // 2
    flat = jnp.concatenate([square[pl.ds(0, half, stride=2), :], square[pl.ds(1, half, stride=2), :]], axis=1)
    for k in range(copies.shape[0]):
        copies[k] = flat


def make_outer(parts, width, receivers, scale):
    return pl.pallas_call(
        functools.partial(outer_kernel, scale=scale),
        out_shape=jax.ShapeDtypeStruct((receivers, width // 2, 2 * width), F32),
        in_specs=[pl.BlockSpec(memory_space=pltpu.VMEM)],
        out_specs=pl.BlockSpec(memory_space=pltpu.VMEM),
        scratch_shapes=[pltpu.VMEM((width, width), F32)],
        compiler_params=pltpu.CompilerParams(vmem_limit_bytes=8 << 20),
        name="outer",
    )(parts)


def pack_kernel(partial, sent, grads, *, tensor, cores, col_rows):
    t = lax.axis_index(TENSOR).astype(jnp.int32)
    core = lax.axis_index("c").astype(jnp.int32)
    each = slot_rows(cores, col_rows)
    squares = []
    for c in range(cores):
        g = partial[c]
        for k in range(1, tensor):
            g = g + partial[k * cores + c]
        grads[c] = g
        squares.append(g * g)
    fill = each - cores * (col_rows + 1)
    total = jnp.broadcast_to(jnp.sum(sum(squares)), (fill, LANES))
    for k in range(sent.shape[0] // each):
        for c in range(cores):
            sent[pl.ds(k * each + c * col_rows, col_rows), :] = grads[c, pl.ds(t * col_rows, col_rows), :]
            sent[pl.ds(k * each + cores * col_rows + c, 1), :] = grads[c, pl.ds(P_ORDER[k] * cores + core, 1), :]
        sent[pl.ds((k + 1) * each - fill, fill), :] = total


def slot_rows(cores, col_rows):
    return cores * col_rows + 4


def make_sent(partial, tensor, cores, chips, col_rows):
    rows = partial.shape[1]
    return pl.pallas_call(
        functools.partial(pack_kernel, tensor=tensor, cores=cores, col_rows=col_rows),
        out_shape=jax.ShapeDtypeStruct((chips * slot_rows(cores, col_rows), LANES), F32),
        in_specs=[pl.BlockSpec(memory_space=pltpu.VMEM)],
        out_specs=pl.BlockSpec(memory_space=pltpu.VMEM),
        scratch_shapes=[pltpu.VMEM((cores, rows, LANES), F32)],
        compiler_params=pltpu.CompilerParams(vmem_limit_bytes=8 << 20),
        name="pack",
    )(partial)


def cov_kernel(got, out, block, sems, *, cores, col_rows, seqs, total_len):
    each = slot_rows(cores, col_rows)
    chips = seqs // cores
    row_begin = lax.axis_index(DP).astype(jnp.int32) * out.shape[0]
    col_begin = lax.axis_index(TENSOR).astype(jnp.int32) * out.shape[1]

    def over_seqs(first, step):
        slots = [got[pl.ds(first + c * step, chips, stride=each), :] for c in range(cores)]
        return jnp.concatenate(slots, axis=0)

    rows = over_seqs(cores * col_rows, 1)
    totals = got[pl.ds(cores * (col_rows + 1), chips, stride=each), :]
    damping = (0.5 / (seqs * total_len)) * jnp.sum(totals, axis=0, keepdims=True)
    row_ids = row_begin + lax.broadcasted_iota(jnp.int32, (out.shape[0], LANES), 0)
    lane_ids = col_begin + lax.broadcasted_iota(jnp.int32, (out.shape[0], LANES), 1)
    copies = []
    for q in range(col_rows):
        raw = lax.dot_general(
            rows, over_seqs(q, col_rows), (((0,), (0,)), ((), ())),
            precision=lax.Precision.HIGHEST, preferred_element_type=F32,
        )
        block[q] = raw * (1.0 / seqs) + jnp.where(row_ids == lane_ids + q * LANES, damping, 0.0)
        copies.append(pltpu.make_async_copy(block.at[q], out.at[:, pl.ds(q * LANES, LANES)], sems.at[q]))
        copies[q].start()
    for copy in copies:
        copy.wait()


def make_cov(got, cores, col_rows, seqs, total_len):
    return pl.pallas_call(
        functools.partial(cov_kernel, cores=cores, col_rows=col_rows, seqs=seqs, total_len=total_len),
        out_shape=jax.ShapeDtypeStruct((LANES, col_rows * LANES), F32),
        in_specs=[pl.BlockSpec(memory_space=pltpu.VMEM)],
        out_specs=pl.BlockSpec(memory_space=pltpu.HBM),
        scratch_shapes=[pltpu.VMEM((col_rows, LANES, LANES), F32), pltpu.SemaphoreType.DMA((col_rows,))],
        compiler_params=pltpu.CompilerParams(vmem_limit_bytes=8 << 20),
        name="cov",
    )(got)


def shards(hidden, grad_out, proj_in, proj_out):
    length = hidden.shape[1]
    width = proj_in.shape[0]
    total_len = width * width
    tensor = lax.axis_size(TENSOR)
    chips = lax.axis_size("p")
    cores = lax.axis_size("c")
    seqs = chips * cores
    col_rows = total_len // tensor // LANES
    each = slot_rows(cores, col_rows)

    panels = make_panels(*(pltpu.with_memory_space_constraint(v, pltpu.HBM) for v in (hidden[0], grad_out[0], proj_in, proj_out)))
    parts = lax.all_to_all(panels.reshape(tensor, length // tensor, 2 * width), TENSOR, 0, 0, axis_index_groups=[T_ORDER])
    copies = make_outer(parts, width, tensor * cores, 1.0 / math.sqrt(length))
    partial = lax.all_to_all(copies, (TENSOR, "c"), 0, 0)
    sent = make_sent(partial, tensor, cores, chips, col_rows)
    got = lax.all_to_all(sent.reshape(chips, each // 4, 4, LANES), "p", 0, 0, axis_index_groups=[P_ORDER])
    return make_cov(got.reshape(chips * each, LANES), cores, col_rows, seqs, total_len)


def solution(mesh):
    fine = Mesh(mesh.devices.reshape(16, 2, 8), ("p", "c", "t"))
    placed = (
        P(DP, None, TENSOR),
        P(DP, None, TENSOR),
        P(None, TENSOR),
        P(None, TENSOR),
    )
    return jax.shard_map(
        shards, mesh=fine, in_specs=placed, out_specs=P(DP, TENSOR), check_vma=False
    )
```

```python
import functools
import math

import jax
import jax.numpy as jnp
from jax import lax
from jax.experimental import pallas as pl
from jax.experimental.pallas import tpu as pltpu
from jax.sharding import Mesh, PartitionSpec as P

DP = ("p", "c")
TENSOR = "t"
LANES = 128
P_ORDER = [10, 0, 1, 3, 2, 4, 5, 7, 6, 12, 8, 13, 15, 14, 9, 11]
T_ORDER = [5, 7, 4, 3, 6, 2, 1, 0]
A_ORDER = [11, 0, 1, 2, 3, 4, 5, 6, 7, 8, 9, 10, 12, 13, 14, 15]
GRAD_BLOCKS = (512, 512)
HIDDEN_BLOCKS = (1536, 1024, 1024)
AHEAD = 3
ROWS = 256
VMEM_LIMIT = 25165824
F32 = jnp.float32


def panels_kernel(hidden, grad_out, proj_in, proj_out, panels, h_buf, g_buf, p_buf, q_buf, sems, proj_sems):
    width = proj_in.shape[0]
    across = (((1,), (1,)), ((), ()))
    proj_copies = (
        pltpu.make_async_copy(proj_out, q_buf, proj_sems.at[0]),
        pltpu.make_async_copy(proj_in, p_buf, proj_sems.at[1]),
    )
    work = []
    for source, buf, proj, lanes, eighths in (
        (grad_out, g_buf, q_buf, pl.ds(width, width), GRAD_BLOCKS),
        (hidden, h_buf, p_buf, pl.ds(0, width), HIDDEN_BLOCKS),
    ):
        begin = 0
        for size in eighths:
            span = pl.ds(begin, size)
            copy = pltpu.make_async_copy(source.at[:, span], buf.at[:, span], sems.at[len(work)])
            work.append((copy, buf, proj, lanes, span, begin == 0))
            begin += size
        assert begin == source.shape[1]
    for copy in proj_copies:
        copy.start()
    for item in work[:AHEAD]:
        item[0].start()
    for copy in proj_copies:
        copy.wait()
    for k, (copy, buf, proj, lanes, span, first) in enumerate(work):
        copy.wait()
        if k + AHEAD < len(work):
            work[k + AHEAD][0].start()
        for r in range(0, panels.shape[0], ROWS):
            rows = pl.ds(r, ROWS)
            part = lax.dot_general(buf[rows, span], proj[:, span], across, preferred_element_type=F32)
            panels[rows, lanes] = part if first else panels[rows, lanes] + part


def make_panels(hidden, grad_out, proj_in, proj_out):
    length, units = hidden.shape
    features = grad_out.shape[1]
    width = proj_in.shape[0]
    blocks = len(GRAD_BLOCKS) + len(HIDDEN_BLOCKS)
    hbm = pl.BlockSpec(memory_space=pltpu.HBM)
    return pl.pallas_call(
        panels_kernel,
        out_shape=jax.ShapeDtypeStruct((length, 2 * width), F32),
        in_specs=[hbm] * 4,
        out_specs=pl.BlockSpec(memory_space=pltpu.VMEM),
        scratch_shapes=[
            pltpu.VMEM((length, units), jnp.bfloat16),
            pltpu.VMEM((length, features), jnp.bfloat16),
            pltpu.VMEM((width, units), jnp.bfloat16),
            pltpu.VMEM((width, features), jnp.bfloat16),
            pltpu.SemaphoreType.DMA((blocks,)),
            pltpu.SemaphoreType.DMA((2,)),
        ],
        compiler_params=pltpu.CompilerParams(vmem_limit_bytes=VMEM_LIMIT),
        name="panels",
    )(hidden, grad_out, proj_in, proj_out)


def outer_kernel(parts, copies, square, *, scale):
    width = square.shape[0]
    mine = jnp.sum(parts[...], axis=0)
    square[...] = lax.dot_general(
        mine[:, :width], mine[:, width:], (((0,), (0,)), ((), ())),
        precision=lax.Precision.HIGHEST, preferred_element_type=F32,
    ) * scale
    half = width // 2
    flat = jnp.concatenate([square[pl.ds(0, half, stride=2), :], square[pl.ds(1, half, stride=2), :]], axis=1)
    for k in range(copies.shape[0]):
        copies[k] = flat


def make_outer(parts, width, receivers, scale):
    return pl.pallas_call(
        functools.partial(outer_kernel, scale=scale),
        out_shape=jax.ShapeDtypeStruct((receivers, width // 2, 2 * width), F32),
        in_specs=[pl.BlockSpec(memory_space=pltpu.VMEM)],
        out_specs=pl.BlockSpec(memory_space=pltpu.VMEM),
        scratch_shapes=[pltpu.VMEM((width, width), F32)],
        compiler_params=pltpu.CompilerParams(vmem_limit_bytes=8 << 20),
        name="outer",
    )(parts)


def pack_kernel(partial, sent, grads, *, tensor, cores, col_rows):
    t = lax.axis_index(TENSOR).astype(jnp.int32)
    core = lax.axis_index("c").astype(jnp.int32)
    each = slot_rows(cores, col_rows)
    squares = []
    for c in range(cores):
        mine = [k for k, place in enumerate(A_ORDER) if place % cores == c]
        g = partial[mine[0]]
        for k in mine[1:]:
            g = g + partial[k]
        grads[c] = g
        squares.append(g * g)
    fill = each - cores * (col_rows + 1)
    total = jnp.broadcast_to(jnp.sum(sum(squares)), (fill, LANES))
    for k in range(sent.shape[0] // each):
        for c in range(cores):
            sent[pl.ds(k * each + c * col_rows, col_rows), :] = grads[c, pl.ds(t * col_rows, col_rows), :]
            sent[pl.ds(k * each + cores * col_rows + c, 1), :] = grads[c, pl.ds(P_ORDER[k] * cores + core, 1), :]
        sent[pl.ds((k + 1) * each - fill, fill), :] = total


def slot_rows(cores, col_rows):
    return cores * col_rows + 4


def make_sent(partial, tensor, cores, chips, col_rows):
    rows = partial.shape[1]
    return pl.pallas_call(
        functools.partial(pack_kernel, tensor=tensor, cores=cores, col_rows=col_rows),
        out_shape=jax.ShapeDtypeStruct((chips * slot_rows(cores, col_rows), LANES), F32),
        in_specs=[pl.BlockSpec(memory_space=pltpu.VMEM)],
        out_specs=pl.BlockSpec(memory_space=pltpu.VMEM),
        scratch_shapes=[pltpu.VMEM((cores, rows, LANES), F32)],
        compiler_params=pltpu.CompilerParams(vmem_limit_bytes=8 << 20),
        name="pack",
    )(partial)


def cov_kernel(got, out, block, sems, *, cores, col_rows, seqs, total_len):
    each = slot_rows(cores, col_rows)
    chips = seqs // cores
    row_begin = lax.axis_index(DP).astype(jnp.int32) * out.shape[0]
    col_begin = lax.axis_index(TENSOR).astype(jnp.int32) * out.shape[1]

    def over_seqs(first, step):
        slots = [got[pl.ds(first + c * step, chips, stride=each), :] for c in range(cores)]
        return jnp.concatenate(slots, axis=0)

    rows = over_seqs(cores * col_rows, 1)
    totals = got[pl.ds(cores * (col_rows + 1), chips, stride=each), :]
    damping = (0.5 / (seqs * total_len)) * jnp.sum(totals, axis=0, keepdims=True)
    row_ids = row_begin + lax.broadcasted_iota(jnp.int32, (out.shape[0], LANES), 0)
    lane_ids = col_begin + lax.broadcasted_iota(jnp.int32, (out.shape[0], LANES), 1)
    copies = []
    for q in range(col_rows):
        raw = lax.dot_general(
            rows, over_seqs(q, col_rows), (((0,), (0,)), ((), ())),
            precision=lax.Precision.HIGHEST, preferred_element_type=F32,
        )
        block[q] = raw * (1.0 / seqs) + jnp.where(row_ids == lane_ids + q * LANES, damping, 0.0)
        copies.append(pltpu.make_async_copy(block.at[q], out.at[:, pl.ds(q * LANES, LANES)], sems.at[q]))
        copies[q].start()
    for copy in copies:
        copy.wait()


def make_cov(got, cores, col_rows, seqs, total_len):
    return pl.pallas_call(
        functools.partial(cov_kernel, cores=cores, col_rows=col_rows, seqs=seqs, total_len=total_len),
        out_shape=jax.ShapeDtypeStruct((LANES, col_rows * LANES), F32),
        in_specs=[pl.BlockSpec(memory_space=pltpu.VMEM)],
        out_specs=pl.BlockSpec(memory_space=pltpu.HBM),
        scratch_shapes=[pltpu.VMEM((col_rows, LANES, LANES), F32), pltpu.SemaphoreType.DMA((col_rows,))],
        compiler_params=pltpu.CompilerParams(vmem_limit_bytes=8 << 20),
        name="cov",
    )(got)


def shards(hidden, grad_out, proj_in, proj_out):
    length = hidden.shape[1]
    width = proj_in.shape[0]
    total_len = width * width
    tensor = lax.axis_size(TENSOR)
    chips = lax.axis_size("p")
    cores = lax.axis_size("c")
    seqs = chips * cores
    col_rows = total_len // tensor // LANES
    each = slot_rows(cores, col_rows)

    panels = make_panels(*(pltpu.with_memory_space_constraint(v, pltpu.HBM) for v in (hidden[0], grad_out[0], proj_in, proj_out)))
    parts = lax.all_to_all(panels.reshape(tensor, length // tensor, 2 * width), TENSOR, 0, 0, axis_index_groups=[T_ORDER])
    copies = make_outer(parts, width, tensor * cores, 1.0 / math.sqrt(length))
    partial = lax.all_to_all(copies, (TENSOR, "c"), 0, 0, axis_index_groups=[A_ORDER])
    sent = make_sent(partial, tensor, cores, chips, col_rows)
    got = lax.all_to_all(sent.reshape(chips, each // 4, 4, LANES), "p", 0, 0, axis_index_groups=[P_ORDER])
    return make_cov(got.reshape(chips * each, LANES), cores, col_rows, seqs, total_len)


def solution(mesh):
    fine = Mesh(mesh.devices.reshape(16, 2, 8), ("p", "c", "t"))
    placed = (
        P(DP, None, TENSOR),
        P(DP, None, TENSOR),
        P(None, TENSOR),
        P(None, TENSOR),
    )
    return jax.shard_map(
        shards, mesh=fine, in_specs=placed, out_specs=P(DP, TENSOR), check_vma=False
    )
```

```python
import functools
import math

import jax
import jax.numpy as jnp
from jax import lax
from jax.experimental import pallas as pl
from jax.experimental.pallas import tpu as pltpu
from jax.sharding import Mesh, PartitionSpec as P

DP = ("p", "c")
TENSOR = "t"
LANES = 128
P_ORDER = [10, 0, 1, 2, 3, 4, 5, 6, 7, 8, 9, 11, 12, 13, 14, 15]
T_ORDER = [5, 7, 4, 3, 6, 2, 1, 0]
A_ORDER = [11, 0, 1, 2, 3, 4, 5, 6, 7, 8, 9, 10, 12, 13, 14, 15]
GRAD_BLOCKS = (512, 512)
HIDDEN_BLOCKS = (1536, 1024, 1024)
AHEAD = 3
ROWS = 256
VMEM_LIMIT = 25165824
F32 = jnp.float32


def panels_kernel(hidden, grad_out, proj_in, proj_out, panels, h_buf, g_buf, p_buf, q_buf, sems, proj_sems):
    width = proj_in.shape[0]
    across = (((1,), (1,)), ((), ()))
    proj_copies = (
        pltpu.make_async_copy(proj_out, q_buf, proj_sems.at[0]),
        pltpu.make_async_copy(proj_in, p_buf, proj_sems.at[1]),
    )
    work = []
    for source, buf, proj, lanes, eighths in (
        (grad_out, g_buf, q_buf, pl.ds(width, width), GRAD_BLOCKS),
        (hidden, h_buf, p_buf, pl.ds(0, width), HIDDEN_BLOCKS),
    ):
        begin = 0
        for size in eighths:
            span = pl.ds(begin, size)
            copy = pltpu.make_async_copy(source.at[:, span], buf.at[:, span], sems.at[len(work)])
            work.append((copy, buf, proj, lanes, span, begin == 0))
            begin += size
        assert begin == source.shape[1]
    for copy in proj_copies:
        copy.start()
    for item in work[:AHEAD]:
        item[0].start()
    for copy in proj_copies:
        copy.wait()
    for k, (copy, buf, proj, lanes, span, first) in enumerate(work):
        copy.wait()
        if k + AHEAD < len(work):
            work[k + AHEAD][0].start()
        for r in range(0, panels.shape[0], ROWS):
            rows = pl.ds(r, ROWS)
            part = lax.dot_general(buf[rows, span], proj[:, span], across, preferred_element_type=F32)
            panels[rows, lanes] = part if first else panels[rows, lanes] + part


def make_panels(hidden, grad_out, proj_in, proj_out):
    length, units = hidden.shape
    features = grad_out.shape[1]
    width = proj_in.shape[0]
    blocks = len(GRAD_BLOCKS) + len(HIDDEN_BLOCKS)
    hbm = pl.BlockSpec(memory_space=pltpu.HBM)
    return pl.pallas_call(
        panels_kernel,
        out_shape=jax.ShapeDtypeStruct((length, 2 * width), F32),
        in_specs=[hbm] * 4,
        out_specs=pl.BlockSpec(memory_space=pltpu.VMEM),
        scratch_shapes=[
            pltpu.VMEM((length, units), jnp.bfloat16),
            pltpu.VMEM((length, features), jnp.bfloat16),
            pltpu.VMEM((width, units), jnp.bfloat16),
            pltpu.VMEM((width, features), jnp.bfloat16),
            pltpu.SemaphoreType.DMA((blocks,)),
            pltpu.SemaphoreType.DMA((2,)),
        ],
        compiler_params=pltpu.CompilerParams(vmem_limit_bytes=VMEM_LIMIT),
        name="panels",
    )(hidden, grad_out, proj_in, proj_out)


def outer_kernel(parts, copies, square, *, scale):
    width = square.shape[0]
    mine = jnp.sum(parts[...], axis=0)
    square[...] = lax.dot_general(
        mine[:, :width], mine[:, width:], (((0,), (0,)), ((), ())),
        precision=lax.Precision.HIGH, preferred_element_type=F32,
    ) * scale
    half = width // 2
    flat = jnp.concatenate([square[pl.ds(0, half, stride=2), :], square[pl.ds(1, half, stride=2), :]], axis=1)
    for k in range(copies.shape[0]):
        copies[k] = flat


def make_outer(parts, width, receivers, scale):
    return pl.pallas_call(
        functools.partial(outer_kernel, scale=scale),
        out_shape=jax.ShapeDtypeStruct((receivers, width // 2, 2 * width), F32),
        in_specs=[pl.BlockSpec(memory_space=pltpu.VMEM)],
        out_specs=pl.BlockSpec(memory_space=pltpu.VMEM),
        scratch_shapes=[pltpu.VMEM((width, width), F32)],
        compiler_params=pltpu.CompilerParams(vmem_limit_bytes=8 << 20),
        name="outer",
    )(parts)


def pack_kernel(partial, sent, grads, *, tensor, cores, col_rows):
    t = lax.axis_index(TENSOR).astype(jnp.int32)
    core = lax.axis_index("c").astype(jnp.int32)
    each = slot_rows(cores, col_rows)
    squares = []
    for c in range(cores):
        mine = [k for k, place in enumerate(A_ORDER) if place % cores == c]
        g = partial[mine[0]]
        for k in mine[1:]:
            g = g + partial[k]
        grads[c] = g
        squares.append(g * g)
    fill = each - cores * (col_rows + 1)
    total = jnp.broadcast_to(jnp.sum(sum(squares)), (fill, LANES))
    for k in range(sent.shape[0] // each):
        for c in range(cores):
            sent[pl.ds(k * each + c * col_rows, col_rows), :] = grads[c, pl.ds(t * col_rows, col_rows), :]
            sent[pl.ds(k * each + cores * col_rows + c, 1), :] = grads[c, pl.ds(P_ORDER[k] * cores + core, 1), :]
        sent[pl.ds((k + 1) * each - fill, fill), :] = total


def slot_rows(cores, col_rows):
    return cores * col_rows + 4


def make_sent(partial, tensor, cores, chips, col_rows):
    rows = partial.shape[1]
    return pl.pallas_call(
        functools.partial(pack_kernel, tensor=tensor, cores=cores, col_rows=col_rows),
        out_shape=jax.ShapeDtypeStruct((chips * slot_rows(cores, col_rows), LANES), F32),
        in_specs=[pl.BlockSpec(memory_space=pltpu.VMEM)],
        out_specs=pl.BlockSpec(memory_space=pltpu.VMEM),
        scratch_shapes=[pltpu.VMEM((cores, rows, LANES), F32)],
        compiler_params=pltpu.CompilerParams(vmem_limit_bytes=8 << 20),
        name="pack",
    )(partial)


def cov_kernel(got, out, block, sems, *, cores, col_rows, seqs, total_len):
    each = slot_rows(cores, col_rows)
    chips = seqs // cores
    row_begin = lax.axis_index(DP).astype(jnp.int32) * out.shape[0]
    col_begin = lax.axis_index(TENSOR).astype(jnp.int32) * out.shape[1]

    def over_seqs(first, step):
        slots = [got[pl.ds(first + c * step, chips, stride=each), :] for c in range(cores)]
        return jnp.concatenate(slots, axis=0)

    rows = over_seqs(cores * col_rows, 1)
    totals = got[pl.ds(cores * (col_rows + 1), chips, stride=each), :]
    damping = (0.5 / (seqs * total_len)) * jnp.sum(totals, axis=0, keepdims=True)
    row_ids = row_begin + lax.broadcasted_iota(jnp.int32, (out.shape[0], LANES), 0)
    lane_ids = col_begin + lax.broadcasted_iota(jnp.int32, (out.shape[0], LANES), 1)
    copies = []
    for q in range(col_rows):
        raw = lax.dot_general(
            rows, over_seqs(q, col_rows), (((0,), (0,)), ((), ())),
            precision=lax.Precision.HIGH, preferred_element_type=F32,
        )
        block[q] = raw * (1.0 / seqs) + jnp.where(row_ids == lane_ids + q * LANES, damping, 0.0)
        copies.append(pltpu.make_async_copy(block.at[q], out.at[:, pl.ds(q * LANES, LANES)], sems.at[q]))
        copies[q].start()
    for copy in copies:
        copy.wait()


def make_cov(got, cores, col_rows, seqs, total_len):
    return pl.pallas_call(
        functools.partial(cov_kernel, cores=cores, col_rows=col_rows, seqs=seqs, total_len=total_len),
        out_shape=jax.ShapeDtypeStruct((LANES, col_rows * LANES), F32),
        in_specs=[pl.BlockSpec(memory_space=pltpu.VMEM)],
        out_specs=pl.BlockSpec(memory_space=pltpu.HBM),
        scratch_shapes=[pltpu.VMEM((col_rows, LANES, LANES), F32), pltpu.SemaphoreType.DMA((col_rows,))],
        compiler_params=pltpu.CompilerParams(vmem_limit_bytes=8 << 20),
        name="cov",
    )(got)


def shards(hidden, grad_out, proj_in, proj_out):
    length = hidden.shape[1]
    width = proj_in.shape[0]
    total_len = width * width
    tensor = lax.axis_size(TENSOR)
    chips = lax.axis_size("p")
    cores = lax.axis_size("c")
    seqs = chips * cores
    col_rows = total_len // tensor // LANES
    each = slot_rows(cores, col_rows)

    panels = make_panels(*(pltpu.with_memory_space_constraint(v, pltpu.HBM) for v in (hidden[0], grad_out[0], proj_in, proj_out)))
    parts = lax.all_to_all(panels.reshape(tensor, length // tensor, 2 * width), TENSOR, 0, 0, axis_index_groups=[T_ORDER])
    copies = make_outer(parts, width, tensor * cores, 1.0 / math.sqrt(length))
    partial = lax.all_to_all(copies, (TENSOR, "c"), 0, 0, axis_index_groups=[A_ORDER])
    sent = make_sent(partial, tensor, cores, chips, col_rows)
    got = lax.all_to_all(sent.reshape(chips, each // 4, 4, LANES), "p", 0, 0, axis_index_groups=[P_ORDER])
    return make_cov(got.reshape(chips * each, LANES), cores, col_rows, seqs, total_len)


def solution(mesh):
    fine = Mesh(mesh.devices.reshape(16, 2, 8), ("p", "c", "t"))
    placed = (
        P(DP, None, TENSOR),
        P(DP, None, TENSOR),
        P(None, TENSOR),
        P(None, TENSOR),
    )
    return jax.shard_map(
        shards, mesh=fine, in_specs=placed, out_specs=P(DP, TENSOR), check_vma=False
    )
```

```python
import functools
import math

import jax
import jax.numpy as jnp
from jax import lax
from jax.experimental import pallas as pl
from jax.experimental.pallas import tpu as pltpu
from jax.sharding import Mesh, PartitionSpec as P

DP = ("p", "c")
TENSOR = "t"
LANES = 128
P_ORDER = [10, 0, 1, 3, 2, 4, 5, 7, 6, 12, 8, 13, 15, 14, 9, 11]
T_ORDER = [5, 7, 4, 3, 6, 2, 1, 0]
A_ORDER = [11, 0, 1, 2, 3, 4, 5, 6, 7, 8, 9, 10, 12, 13, 14, 15]
GRAD_BLOCKS = (256, 768)
HIDDEN_BLOCKS = (1536, 1280, 768)
AHEAD = 3
ROWS = 256
VMEM_LIMIT = 25165824
F32 = jnp.float32


def panels_kernel(hidden, grad_out, proj_in, proj_out, panels, h_buf, g_buf, p_buf, q_buf, sems, proj_sems):
    width = proj_in.shape[0]
    across = (((1,), (1,)), ((), ()))
    proj_copies = (
        pltpu.make_async_copy(proj_out, q_buf, proj_sems.at[0]),
        pltpu.make_async_copy(proj_in, p_buf, proj_sems.at[1]),
    )
    work = []
    for source, buf, proj, lanes, eighths in (
        (grad_out, g_buf, q_buf, pl.ds(width, width), GRAD_BLOCKS),
        (hidden, h_buf, p_buf, pl.ds(0, width), HIDDEN_BLOCKS),
    ):
        begin = 0
        for size in eighths:
            span = pl.ds(begin, size)
            copy = pltpu.make_async_copy(source.at[:, span], buf.at[:, span], sems.at[len(work)])
            work.append((copy, buf, proj, lanes, span, begin == 0))
            begin += size
        assert begin == source.shape[1]
    for copy in proj_copies:
        copy.start()
    for item in work[:AHEAD]:
        item[0].start()
    for copy in proj_copies:
        copy.wait()
    for k, (copy, buf, proj, lanes, span, first) in enumerate(work):
        copy.wait()
        if k + AHEAD < len(work):
            work[k + AHEAD][0].start()
        for r in range(0, panels.shape[0], ROWS):
            rows = pl.ds(r, ROWS)
            part = lax.dot_general(buf[rows, span], proj[:, span], across, preferred_element_type=F32)
            panels[rows, lanes] = part if first else panels[rows, lanes] + part


def make_panels(hidden, grad_out, proj_in, proj_out):
    length, units = hidden.shape
    features = grad_out.shape[1]
    width = proj_in.shape[0]
    blocks = len(GRAD_BLOCKS) + len(HIDDEN_BLOCKS)
    hbm = pl.BlockSpec(memory_space=pltpu.HBM)
    return pl.pallas_call(
        panels_kernel,
        out_shape=jax.ShapeDtypeStruct((length, 2 * width), F32),
        in_specs=[hbm] * 4,
        out_specs=pl.BlockSpec(memory_space=pltpu.VMEM),
        scratch_shapes=[
            pltpu.VMEM((length, units), jnp.bfloat16),
            pltpu.VMEM((length, features), jnp.bfloat16),
            pltpu.VMEM((width, units), jnp.bfloat16),
            pltpu.VMEM((width, features), jnp.bfloat16),
            pltpu.SemaphoreType.DMA((blocks,)),
            pltpu.SemaphoreType.DMA((2,)),
        ],
        compiler_params=pltpu.CompilerParams(vmem_limit_bytes=VMEM_LIMIT),
        name="panels",
    )(hidden, grad_out, proj_in, proj_out)


def outer_kernel(parts, copies, square, *, scale):
    width = square.shape[0]
    mine = jnp.sum(parts[...], axis=0)
    square[...] = lax.dot_general(
        mine[:, :width], mine[:, width:], (((0,), (0,)), ((), ())),
        precision=lax.Precision.HIGHEST, preferred_element_type=F32,
    ) * scale
    half = width // 2
    flat = jnp.concatenate([square[pl.ds(0, half, stride=2), :], square[pl.ds(1, half, stride=2), :]], axis=1)
    for k in range(copies.shape[0]):
        copies[k] = flat


def make_outer(parts, width, receivers, scale):
    return pl.pallas_call(
        functools.partial(outer_kernel, scale=scale),
        out_shape=jax.ShapeDtypeStruct((receivers, width // 2, 2 * width), F32),
        in_specs=[pl.BlockSpec(memory_space=pltpu.VMEM)],
        out_specs=pl.BlockSpec(memory_space=pltpu.VMEM),
        scratch_shapes=[pltpu.VMEM((width, width), F32)],
        compiler_params=pltpu.CompilerParams(vmem_limit_bytes=8 << 20),
        name="outer",
    )(parts)


def pack_kernel(partial, sent, grads, *, tensor, cores, col_rows):
    t = lax.axis_index(TENSOR).astype(jnp.int32)
    core = lax.axis_index("c").astype(jnp.int32)
    each = slot_rows(cores, col_rows)
    squares = []
    for c in range(cores):
        mine = [k for k, place in enumerate(A_ORDER) if place % cores == c]
        g = partial[mine[0]]
        for k in mine[1:]:
            g = g + partial[k]
        grads[c] = g
        squares.append(g * g)
    fill = each - cores * (col_rows + 1)
    total = jnp.broadcast_to(jnp.sum(sum(squares)), (fill, LANES))
    for k in range(sent.shape[0] // each):
        for c in range(cores):
            sent[pl.ds(k * each + c * col_rows, col_rows), :] = grads[c, pl.ds(t * col_rows, col_rows), :]
            sent[pl.ds(k * each + cores * col_rows + c, 1), :] = grads[c, pl.ds(P_ORDER[k] * cores + core, 1), :]
        sent[pl.ds((k + 1) * each - fill, fill), :] = total


def slot_rows(cores, col_rows):
    return cores * col_rows + 4


def make_sent(partial, tensor, cores, chips, col_rows):
    rows = partial.shape[1]
    return pl.pallas_call(
        functools.partial(pack_kernel, tensor=tensor, cores=cores, col_rows=col_rows),
        out_shape=jax.ShapeDtypeStruct((chips * slot_rows(cores, col_rows), LANES), F32),
        in_specs=[pl.BlockSpec(memory_space=pltpu.VMEM)],
        out_specs=pl.BlockSpec(memory_space=pltpu.VMEM),
        scratch_shapes=[pltpu.VMEM((cores, rows, LANES), F32)],
        compiler_params=pltpu.CompilerParams(vmem_limit_bytes=8 << 20),
        name="pack",
    )(partial)


def cov_kernel(got, out, block, sems, *, cores, col_rows, seqs, total_len):
    each = slot_rows(cores, col_rows)
    chips = seqs // cores
    row_begin = lax.axis_index(DP).astype(jnp.int32) * out.shape[0]
    col_begin = lax.axis_index(TENSOR).astype(jnp.int32) * out.shape[1]

    def over_seqs(first, step):
        slots = [got[pl.ds(first + c * step, chips, stride=each), :] for c in range(cores)]
        return jnp.concatenate(slots, axis=0)

    rows = over_seqs(cores * col_rows, 1)
    totals = got[pl.ds(cores * (col_rows + 1), chips, stride=each), :]
    damping = (0.5 / (seqs * total_len)) * jnp.sum(totals, axis=0, keepdims=True)
    row_ids = row_begin + lax.broadcasted_iota(jnp.int32, (out.shape[0], LANES), 0)
    lane_ids = col_begin + lax.broadcasted_iota(jnp.int32, (out.shape[0], LANES), 1)
    copies = []
    for q in range(col_rows):
        raw = lax.dot_general(
            rows, over_seqs(q, col_rows), (((0,), (0,)), ((), ())),
            precision=lax.Precision.HIGHEST, preferred_element_type=F32,
        )
        block[q] = raw * (1.0 / seqs) + jnp.where(row_ids == lane_ids + q * LANES, damping, 0.0)
        copies.append(pltpu.make_async_copy(block.at[q], out.at[:, pl.ds(q * LANES, LANES)], sems.at[q]))
        copies[q].start()
    for copy in copies:
        copy.wait()


def make_cov(got, cores, col_rows, seqs, total_len):
    return pl.pallas_call(
        functools.partial(cov_kernel, cores=cores, col_rows=col_rows, seqs=seqs, total_len=total_len),
        out_shape=jax.ShapeDtypeStruct((LANES, col_rows * LANES), F32),
        in_specs=[pl.BlockSpec(memory_space=pltpu.VMEM)],
        out_specs=pl.BlockSpec(memory_space=pltpu.HBM),
        scratch_shapes=[pltpu.VMEM((col_rows, LANES, LANES), F32), pltpu.SemaphoreType.DMA((col_rows,))],
        compiler_params=pltpu.CompilerParams(vmem_limit_bytes=8 << 20),
        name="cov",
    )(got)


def shards(hidden, grad_out, proj_in, proj_out):
    length = hidden.shape[1]
    width = proj_in.shape[0]
    total_len = width * width
    tensor = lax.axis_size(TENSOR)
    chips = lax.axis_size("p")
    cores = lax.axis_size("c")
    seqs = chips * cores
    col_rows = total_len // tensor // LANES
    each = slot_rows(cores, col_rows)

    panels = make_panels(*(pltpu.with_memory_space_constraint(v, pltpu.HBM) for v in (hidden[0], grad_out[0], proj_in, proj_out)))
    parts = lax.all_to_all(panels.reshape(tensor, length // tensor, 2 * width), TENSOR, 0, 0, axis_index_groups=[T_ORDER])
    copies = make_outer(parts, width, tensor * cores, 1.0 / math.sqrt(length))
    partial = lax.all_to_all(copies, (TENSOR, "c"), 0, 0, axis_index_groups=[A_ORDER])
    sent = make_sent(partial, tensor, cores, chips, col_rows)
    got = lax.all_to_all(sent.reshape(chips, each // 4, 4, LANES), "p", 0, 0, axis_index_groups=[P_ORDER])
    return make_cov(got.reshape(chips * each, LANES), cores, col_rows, seqs, total_len)


def solution(mesh):
    fine = Mesh(mesh.devices.reshape(16, 2, 8), ("p", "c", "t"))
    placed = (
        P(DP, None, TENSOR),
        P(DP, None, TENSOR),
        P(None, TENSOR),
        P(None, TENSOR),
    )
    return jax.shard_map(
        shards, mesh=fine, in_specs=placed, out_specs=P(DP, TENSOR), check_vma=False
    )
```
